32 devices in a mesh: pool: 2 (over x), node: 16 (over z, y, core), local: 1.
Axes of the slice: x: 2, y: 2, z: 4, core: 2. Of those that a mesh axis runs over, the one named last changes fastest.
Arguments:
- tokens: bfloat16 [512, 3584], P(('pool', 'node', 'local')), parts along dimension 0, may hold values from -6 to 6
- routes: int32 [512, 8], P(('pool', 'node', 'local')), parts along dimension 0, may hold values from 0 to 15, all different within a row; in each aligned block of 16 rows (0 to 15, 16 to 31, ...) at most 16 rows name the same one
- route_weights: int32 [512, 8], P(('pool', 'node', 'local')), parts along dimension 0, may hold values from 1 to 256
- placement: int32 [16], replicated, may hold values from 0 to 15, each once
- expert_gate: bfloat16 [16, 3584, 1024], P('node', None, 'local'), may hold values from -0.09375 to 0.09375
- expert_up: bfloat16 [16, 3584, 1024], P('node', None, 'local'), may hold values from -0.09375 to 0.09375
- expert_down: bfloat16 [16, 1024, 3584], P('node', 'local'), may hold values from -0.1875 to 0.1875
- shared_gate: bfloat16 [3584, 2048], P(None, 'node'), may hold values from -0.09375 to 0.09375
- shared_up: bfloat16 [3584, 2048], P(None, 'node'), may hold values from -0.09375 to 0.09375
- shared_down: bfloat16 [2048, 3584], P('node'), may hold values from -0.125 to 0.125
Outputs:
- mixed: bfloat16 [512, 3584], P(('pool', 'node', 'local')), parts along dimension 0
The draws below stay inside these ranges and needn't reach their ends.
There are 2 independent parts, one for each index of `pool`. The reference program is written for one: setup_inputs(seed, part) draws one part's arguments, and reference() takes and returns one part's arrays. A program takes and returns all parts, laid end to end along the dimension named above; an argument that names none is the same for every part. Nothing has to cross between parts.
Inputs may be any that keep to these rules, and one draw needn't show every extreme that they name: `routes`: each row names 8 different experts; the 16 rows of one device name one expert at most 16 times, a bound that some block reaches in some devices' rows. `placement`: each slot holds exactly one expert.
All inputs are finite; a program needn't handle non-finite values.
Results may differ from the reference program's by a relative error of at most 0.015.
Values may be sent and summed in bfloat16 or wider, within the bound.
No kernel may reach another device: no remote copies, remote signals or barrier semaphores. Data moves between devices by JAX's collectives and lax.ppermute only.
A program may use at most 128 MiB of HBM per device.

```python
import math
import jax
import jax.numpy as jnp
import numpy as np
from jax import lax

D = 3584
HE = 1024
SHARED = 2048
TOPK = 8
TOK_DEV = 16
EXPERTS = 16
HALF = 1024
SHARED_DEV = 128
CAP = 16
TOKENS = 256
N_NODE = 16
N_LOCAL = 1


def touch_ends(result, rng, least, largest):
    extent = result.shape
    place = [jax.random.randint(jax.random.fold_in(rng, axis), (), 0, extent[axis]) for axis in range(len(extent))]
    result = result.at[tuple(place)].set(least)
    longest = extent.index(max(extent))
    place[longest] = (place[longest] + 1) % extent[longest]
    return result.at[tuple(place)].set(largest)


def levels(rng, dims, cuts, low, largest):
    level = 1.0
    for dim, blocks in cuts:
        steps = jax.random.uniform(jax.random.fold_in(jax.random.fold_in(rng, 6), dim), (blocks,), jnp.float32, low / len(cuts), largest / len(cuts))
        level = level * jnp.repeat(jnp.exp(steps), dims[dim] // blocks).reshape((-1,) + (1,) * (len(dims) - 1 - dim))
    return level


def routed_block(stream_key, own, number, rows, number_of, top, limit, slope):
    order = jax.random.permutation(stream_key, number_of)
    packed, common = load_shares(number_of, rows * top, limit, slope, True), load_shares(number_of, rows * top, limit, slope, False)
    places = jnp.arange(number_of)

    def named(sizes, offset_by):
        used = int((sizes > 0).sum())
        fixed = max(1, used // 4)
        moved = fixed + (places - fixed + offset_by * (used - fixed)) % max(1, number_of - fixed)
        return jnp.zeros((number_of,), jnp.int32).at[order[jnp.where(places < fixed, places, moved)]].set(jnp.asarray(sizes, jnp.int32))

    sizes = jnp.where(number % 4 == 0, named(packed, number // 4), named(common, number - number // 4 - 1))
    mixed = jax.random.permutation(jax.random.fold_in(own, 3), number_of)
    donor, taker = mixed[0:number_of // 2 * 2:2], mixed[1:number_of // 2 * 2:2]
    margin = jnp.minimum(sizes[donor] - 1, limit - sizes[taker]) // 2
    margin = jnp.where((donor == order[0]) | (taker == order[0]) | (sizes[taker] == 0), 0, jnp.maximum(margin, 0))
    moved = jax.random.randint(jax.random.fold_in(own, 4), (number_of // 2,), 0, 1 << 20) % (margin + 1)
    sizes = sizes.at[donor].add(-moved).at[taker].add(moved)
    items = jnp.searchsorted(jnp.cumsum(sizes), jnp.arange(rows * top), side="right").astype(jnp.int32)
    table = items.reshape(top, rows).T
    table = table[jax.random.permutation(jax.random.fold_in(own, 1), rows)]
    offset_by = jax.random.randint(jax.random.fold_in(own, 2), (rows, 1), 0, top)
    return jnp.take_along_axis(table, (jnp.arange(top)[None, :] + offset_by) % top, axis=1)


def load_shares(count, total, most, lean, full):
    loads = [(1 << 20) // math.isqrt(grade ** lean) + 1 for grade in range(1, count + 1)]
    largest = most if full else min(most, max(-(-total // count), total * loads[0] // sum(loads)))
    least = 1 if total - largest >= count - 1 else 0
    counts, spare = [largest] + [least] * (count - 1), total - largest - least * (count - 1)
    while spare > 0:
        free = [i for i in range(1, count) if counts[i] < largest] or [i for i in range(1, count) if counts[i] < most]
        mass, remaining = sum([loads[i] for i in free]), spare
        for i in free:
            more = min(most - counts[i], max(1, remaining * loads[i] // mass), spare)
            counts[i] = counts[i] + more
            spare = spare - more
    return np.array(counts)


def bell_draw(rng, dims, deviation, reach, split=(), kind=jnp.bfloat16):
    entries = deviation * jax.random.normal(rng, dims, jnp.float32)
    if split:
        entries = entries * levels(rng, dims, split, -0.22, 0.18)
    return jnp.clip(entries, -reach, reach).astype(kind)


def setup_inputs(seed: int = 0, part: int = 0) -> dict:
    arg_keys = jax.random.split(jax.random.key(seed), 11)
    part_keys = jax.random.split(jax.random.fold_in(arg_keys[10], part), 11)
    tokens = bell_draw(part_keys[0], (TOKENS, D), 1.0, 6.0, ((0, 16),))
    routes_keys = jax.random.split(jax.random.fold_in(part_keys[1], 1), TOKENS // TOK_DEV)
    routes_turns = jax.random.permutation(jax.random.fold_in(part_keys[1], 3), TOKENS // TOK_DEV)
    routes = jax.vmap(lambda own, number: routed_block(jax.random.fold_in(part_keys[1], 2), own, number, TOK_DEV, EXPERTS, TOPK, CAP, 2))(routes_keys, routes_turns).reshape((TOKENS, TOPK))
    route_weights = touch_ends(jax.random.randint(part_keys[2], (TOKENS, TOPK), 1, 257), jax.random.fold_in(part_keys[2], 1), 1, 256).astype(jnp.int32)
    placement = jax.random.permutation(arg_keys[3], EXPERTS).astype(jnp.int32)
    expert_gate = bell_draw(arg_keys[4], (EXPERTS, D, HE), D ** -0.5, 0.09375, ((0, 16),))
    expert_up = bell_draw(arg_keys[5], (EXPERTS, D, HE), D ** -0.5, 0.09375, ((0, 16),))
    expert_down = bell_draw(arg_keys[6], (EXPERTS, HE, D), HE ** -0.5, 0.1875, ((0, 16),))
    shared_gate = bell_draw(arg_keys[7], (D, SHARED), D ** -0.5, 0.09375, ((1, 16),))
    shared_up = bell_draw(arg_keys[8], (D, SHARED), D ** -0.5, 0.09375, ((1, 16),))
    shared_down = bell_draw(arg_keys[9], (SHARED, D), SHARED ** -0.5, 0.125, ((0, 16),))
    return {"tokens": tokens, "routes": routes, "route_weights": route_weights, "placement": placement, "expert_gate": expert_gate, "expert_up": expert_up, "expert_down": expert_down, "shared_gate": shared_gate, "shared_up": shared_up, "shared_down": shared_down}


gain_scale = 1.0 / 256.0


def reference(tokens, routes, route_weights, placement, expert_gate, expert_up, expert_down, shared_gate, shared_up, shared_down):
    slot_width = N_NODE * N_LOCAL * CAP
    chip_slot = placement[routes].astype(jnp.int32).reshape(-1)
    gains = route_weights.astype(jnp.float32).reshape(-1) * gain_scale
    token_of_pair = (jnp.arange(TOKENS * TOPK, dtype=jnp.int32) // TOPK).astype(jnp.int32)

    def per_chip(running, chip):
        matched = chip_slot == chip
        position = (jnp.cumsum(matched.astype(jnp.int32)) - 1).astype(jnp.int32)
        position = jnp.where(matched, position, slot_width).astype(jnp.int32)
        token_slot = jnp.zeros((slot_width,), jnp.int32).at[position].set(token_of_pair, mode="drop")
        slot_gain = jnp.zeros((slot_width,), jnp.float32).at[position].set(gains, mode="drop")
        gathered = tokens[token_slot]
        gate_act = jnp.dot(gathered, expert_gate[chip], preferred_element_type=jnp.float32)
        up_act = jnp.dot(gathered, expert_up[chip], preferred_element_type=jnp.float32)
        hidden = (jax.nn.silu(gate_act) * up_act).astype(jnp.bfloat16)
        down_rows = expert_down[chip]
        summed = jnp.zeros((slot_width, D), jnp.float32)
        for group_index in range(N_LOCAL):
            part_rows = jnp.dot(hidden[:, group_index * HALF:(group_index + 1) * HALF], down_rows[group_index * HALF:(group_index + 1) * HALF], preferred_element_type=jnp.float32)
            summed = summed + lax.optimization_barrier(part_rows.astype(jnp.bfloat16)).astype(jnp.float32)
        expert_out = lax.optimization_barrier(summed.astype(jnp.bfloat16)).astype(jnp.float32)
        running = running.at[token_slot].add(slot_gain[:, None] * expert_out)
        return running, None

    routed, unused = lax.scan(per_chip, jnp.zeros((TOKENS, D), jnp.float32), jnp.arange(N_NODE, dtype=jnp.int32))
    shared_gate_act = jnp.dot(tokens, shared_gate, preferred_element_type=jnp.float32)
    shared_up_act = jnp.dot(tokens, shared_up, preferred_element_type=jnp.float32)
    shared_hidden = (jax.nn.silu(shared_gate_act) * shared_up_act).astype(jnp.bfloat16)
    hidden_groups = shared_hidden.reshape(TOKENS, N_NODE, SHARED_DEV)
    down_groups = shared_down.reshape(N_NODE, SHARED_DEV, D)

    def add_group(total, group):
        hidden_part = lax.dynamic_index_in_dim(hidden_groups, group, 1, keepdims=False)
        down_part = lax.dynamic_index_in_dim(down_groups, group, 0, keepdims=False)
        part_rows = jnp.dot(hidden_part, down_part, preferred_element_type=jnp.float32)
        return total + lax.optimization_barrier(part_rows.astype(jnp.bfloat16)).astype(jnp.float32), None

    shared, unused_two = lax.scan(add_group, jnp.zeros((TOKENS, D), jnp.float32), jnp.arange(N_NODE, dtype=jnp.int32))
    return (routed + shared).astype(jnp.bfloat16)
```

```python
import jax
import jax.numpy as jnp
from jax import lax
from jax.sharding import PartitionSpec as P

gain_scale = 1.0 / 256.0
LANES = 128


def peers(flip, count):
    return [(device, device ^ flip) for device in range(count)]


def shards(
    tokens,
    routes,
    route_weights,
    placement,
    expert_gate,
    expert_up,
    expert_down,
    shared_gate,
    shared_up,
    shared_down,
):
    node_count = lax.axis_size("node")
    core_count = lax.axis_size("local")
    tok_count, model_width = tokens.shape
    device_count = node_count * core_count
    assert device_count & (device_count - 1) == 0
    flips = [1 << bit for bit in range(device_count.bit_length() - 1)]
    inner = max(1, core_count.bit_length() - 1)
    axes = ("node", "local")

    def swap(rows, flip):
        return lax.ppermute(rows, axes, peers(flip, device_count))

    slots = lax.broadcasted_iota(jnp.int32, (1, 1, node_count), 2)
    chip_slot = jnp.sum(
        jnp.where(routes[:, :, None] == slots, placement[None, None, :], 0), axis=2
    )
    gains = jnp.sum(
        jnp.where(
            chip_slot[:, :, None] == slots,
            route_weights.astype(jnp.float32)[:, :, None] * gain_scale,
            0.0,
        ),
        axis=1,
    ).astype(jnp.bfloat16)
    gain_width = -(-node_count // LANES) * LANES
    gains = jnp.pad(gains, ((0, 0), (0, gain_width - node_count)))
    own = jnp.concatenate([tokens, gains], axis=1)

    axis_y, axis_l, axis_h = flips[inner : inner + 3]
    rest = flips[inner + 3 :] + flips[:inner]
    row_y, row_l, row_h = swap(own, axis_y), swap(own, axis_l), swap(own, axis_h)
    row_lh = swap(row_h, axis_l)
    row_ly_hy = swap(jnp.concatenate([row_l, row_h]), axis_y)
    row_lhy = swap(row_lh, axis_y)
    rows = jnp.concatenate([own, row_y, row_l, row_h, row_lh, row_ly_hy, row_lhy])
    for flip in rest:
        rows = jnp.concatenate([rows, swap(rows, flip)])

    x = rows[:, :model_width]
    slot = lax.axis_index("node")
    my_gain = jnp.sum(
        jnp.where(
            lax.broadcasted_iota(jnp.int32, (1, gain_width), 1) == slot,
            rows[:, model_width:].astype(jnp.float32),
            0.0,
        ),
        axis=1,
        keepdims=True,
    )
    gate_act = jnp.dot(x, expert_gate[0], preferred_element_type=jnp.float32)
    up_act = jnp.dot(x, expert_up[0], preferred_element_type=jnp.float32)
    hidden = (jax.nn.silu(gate_act) * up_act * my_gain).astype(jnp.bfloat16)
    shared_gate_act = jnp.dot(x, shared_gate, preferred_element_type=jnp.float32)
    shared_up_act = jnp.dot(x, shared_up, preferred_element_type=jnp.float32)
    shared_hidden = jax.nn.silu(shared_gate_act) * shared_up_act
    if core_count > 1:
        row = lax.broadcasted_iota(jnp.int32, (rows.shape[0], 1), 0)
        shared_hidden = jnp.where(row < tok_count * node_count, shared_hidden, 0.0)
    shared_hidden = shared_hidden.astype(jnp.bfloat16)
    parts = jnp.dot(hidden, expert_down[0], preferred_element_type=jnp.float32)
    parts += jnp.dot(shared_hidden, shared_down, preferred_element_type=jnp.float32)

    def wide(rows):
        return rows.astype(jnp.float32)

    def narrow(rows):
        return rows.astype(jnp.bfloat16)

    sums = parts
    for flip in reversed(rest):
        half = sums.shape[0] // 2
        sums = sums[:half] + wide(swap(narrow(sums[half:]), flip))
    own, sum_y, sum_l, sum_h, sum_lh, sum_ly, sum_hy, sum_lhy = jnp.split(sums, 8)
    sum_lh += wide(swap(narrow(sum_lhy), axis_y))
    back = wide(swap(narrow(jnp.concatenate([sum_ly, sum_hy])), axis_y))
    sum_l += back[:tok_count]
    sum_h += back[tok_count:]
    sum_h += wide(swap(narrow(sum_lh), axis_l))
    own += wide(swap(narrow(sum_y), axis_y))
    own += wide(swap(narrow(sum_l), axis_l))
    own += wide(swap(narrow(sum_h), axis_h))
    return narrow(own)


def solution(mesh):
    placed = (
        P(("pool", "node", "local"), None),
        P(("pool", "node", "local"), None),
        P(("pool", "node", "local"), None),
        P(),
        P("node", None, "local"),
        P("node", None, "local"),
        P("node", "local", None),
        P(None, "node"),
        P(None, "node"),
        P("node", None),
    )
    return jax.shard_map(
        shards,
        mesh=mesh,
        in_specs=placed,
        out_specs=P(("pool", "node", "local"), None),
        check_vma=False,
    )
```
